32 devices in a mesh: lat: 8 (over y, x, core), lon: 4 (over z).
Axes of the slice: x: 2, y: 2, z: 4, core: 2. Of those that a mesh axis runs over, the one named last changes fastest.
Arguments:
- fields: bfloat16 [2, 144, 48, 512], P(None, 'lat', 'lon'), may hold values from -8 to 8
- tangent_pick: int32 [2, 144, 48], P(None, 'lat', 'lon'), may hold values from 0 to 511
- key_mask: int32 [2, 144, 48], P(None, 'lat', 'lon'), may hold values 0 or 1
- w_qkv: bfloat16 [2, 512, 1536], P(None, 'lon'), may hold values from -0.25 to 0.25
- w_out: bfloat16 [2, 512, 512], P(None, 'lon'), may hold values from -0.25 to 0.25
- w_up: bfloat16 [2, 512, 2048], P(None, 'lon'), may hold values from -0.25 to 0.25
- w_down: bfloat16 [2, 2048, 512], P(None, 'lon'), may hold values from -0.125 to 0.125
Outputs:
- primal_out: bfloat16 [2, 144, 48, 512], P(None, 'lat', 'lon')
- tangent_out: bfloat16 [2, 144, 48, 512], P(None, 'lat', 'lon')
The draws below stay inside these ranges and needn't reach their ends.
All inputs are finite; a program needn't handle non-finite values. No bound on the sum of `key_mask` on one device may be relied on, other than what follows from the above.
Results may differ from the reference program's by a relative error of at most 0.03.
Values may be sent and summed in bfloat16 or wider, within the bound.
No kernel may reach another device: no remote copies, remote signals or barrier semaphores. Data moves between devices by JAX's collectives and lax.ppermute only.
A program may use at most 128 MiB of HBM per device.

```python
import jax
import jax.numpy as jnp
from jax import lax

D = 512
HEADS = 8
FF = 2048
LEV = 2
WLAT = 6
WLON = 12
NLAT = 144
NLON = 48


def draw_fields(key, part):
    shape = (LEV, NLAT, NLON, D)
    values = jax.random.truncated_normal(key, -6.0, 6.0, shape, jnp.float32)
    return values.astype(jnp.bfloat16)


def place_ends(values, stream_key, low, high):
    longest = values.shape.index(max(values.shape))
    spots = []
    for shift in (0, 1):
        where = [jax.random.randint(jax.random.fold_in(stream_key, axis), (), 0, length) for axis, length in enumerate(values.shape)]
        where[longest] = (where[longest] + shift) % values.shape[longest]
        spots.append(tuple(where))
    return values.at[spots[0]].set(low).at[spots[1]].set(high)


def steps_of(key, shape, split, smallest, top_value):
    def one(dim, parts):
        steps = jax.random.uniform(jax.random.fold_in(jax.random.fold_in(key, 6), dim), (parts,), jnp.float32, smallest / len(split), top_value / len(split))
        return jnp.repeat(jnp.exp(steps), shape[dim] // parts).reshape((-1,) + (1,) * (len(shape) - dim - 1))

    factor_of = one(*split[0])
    for cut in split[1:]:
        factor_of = factor_of * one(*cut)
    return factor_of


def noise(rng, shape, width, reach, shards=(), held_as=jnp.bfloat16):
    entries = jax.random.normal(rng, shape, jnp.float32) * width
    if len(shards) > 0:
        entries = steps_of(rng, shape, shards, -0.22, 0.18) * entries
    return jnp.clip(entries, min=-reach, max=reach).astype(held_as)


def setup_inputs(seed: int = 0) -> dict:
    streams_of = jax.random.split(jax.random.key(seed), 8)
    return {
        "fields": draw_fields(jax.random.fold_in(streams_of[7], 71), 0),
        "tangent_pick": place_ends(jax.random.randint(streams_of[1], (LEV, NLAT, NLON), 0, D), jax.random.fold_in(streams_of[1], 1), 0, D - 1).astype(jnp.int32),
        "key_mask": place_ends((jax.random.randint(streams_of[2], (LEV, NLAT, NLON), 0, 8) < 7).astype(jnp.int32), jax.random.fold_in(streams_of[2], 1), 0, 1),
        "w_qkv": noise(streams_of[3], (2, D, 3 * D), D ** -0.5, 0.25, ((1, 4),)),
        "w_out": noise(streams_of[4], (2, D, D), D ** -0.5, 0.25, ((1, 4),)),
        "w_up": noise(streams_of[5], (2, D, FF), D ** -0.5, 0.25, ((1, 4),)),
        "w_down": noise(streams_of[6], (2, FF, D), FF ** -0.5, 0.125, ((1, 4),)),
    }


norm_epsilon = 1e-05

def layer_norm(values):
    center = lax.optimization_barrier(jnp.mean(values, -1, keepdims=True))
    spread = lax.optimization_barrier(jnp.mean(jnp.square(values - center), -1, keepdims=True))
    return (values - center) * lax.rsqrt(spread + norm_epsilon)

def window_attention(packed, usable, region):
    windows, window_len, triple = packed.shape
    model_width = triple // 3
    head_size = model_width // HEADS
    queries = packed[..., :model_width].reshape(windows, window_len, HEADS, head_size).astype(jnp.float32)
    keys_all = packed[..., model_width:2 * model_width].reshape(windows, window_len, HEADS, head_size).astype(jnp.float32)
    values_all = packed[..., 2 * model_width:].reshape(windows, window_len, HEADS, head_size).astype(jnp.float32)
    scores = jnp.einsum('wqhe,wkhe->whqk', queries, keys_all) * head_size ** (-0.5)
    matched = region[:, :, None] == region[:, None, :]
    allowed = (usable[:, None, :] > 0) & matched
    self_pair = jnp.eye(window_len, dtype=bool)
    allowed = allowed | self_pair[None]
    scores = jnp.where(allowed[:, None], scores, -1000000000.0)
    highest = lax.stop_gradient(lax.optimization_barrier(jnp.max(scores, -1, keepdims=True)))
    raised = jnp.exp(scores - highest)
    probs = (raised / lax.optimization_barrier(jnp.sum(raised, -1, keepdims=True))).astype(jnp.bfloat16)
    mixed = jnp.einsum('whqk,wkhe->wqhe', probs.astype(jnp.float32), values_all)
    return mixed.astype(jnp.bfloat16).reshape(windows, window_len, model_width)

def block_tokens(tokens, usable, region, qkv_matrix, out_matrix, up_matrix, down_matrix):
    windows, window_len, model_width = tokens.shape
    flat = tokens.reshape(-1, model_width)
    packed = jnp.dot(flat, qkv_matrix, preferred_element_type=jnp.float32).astype(jnp.bfloat16)
    attended = window_attention(packed.reshape(windows, window_len, -1), usable, region).reshape(-1, model_width)
    projected = jnp.dot(attended, out_matrix, preferred_element_type=jnp.float32)
    hidden = flat.astype(jnp.float32) + layer_norm(projected)
    up_proj = jnp.dot(hidden.astype(jnp.bfloat16), up_matrix, preferred_element_type=jnp.float32)
    activated = jax.nn.gelu(up_proj, approximate=False).astype(jnp.bfloat16)
    down_proj = jnp.dot(activated, down_matrix, preferred_element_type=jnp.float32)
    return (hidden + layer_norm(down_proj)).astype(jnp.bfloat16).reshape(windows, window_len, model_width)

def to_bands(array):
    shaped = array.reshape((LEV, NLAT // WLAT, WLAT) + array.shape[2:])
    return jnp.moveaxis(shaped, 1, 0)

def from_bands(array):
    return jnp.moveaxis(array, 0, 1).reshape((LEV, NLAT) + array.shape[3:])

def band_windows(array):
    trailing = array.shape[3:]
    shaped = array.reshape((LEV, WLAT, NLON // WLON, WLON) + trailing)
    return jnp.moveaxis(shaped, 2, 0).reshape((NLON // WLON, LEV * WLAT * WLON) + trailing)

def band_grid(array):
    shaped = array.reshape((NLON // WLON, LEV, WLAT, WLON) + array.shape[2:])
    return jnp.moveaxis(shaped, 0, 2).reshape((LEV, WLAT, NLON) + array.shape[2:])

def apply_block(primal, tangent, usable, region, matrices):

    def band_pass(inputs):
        band_primal, band_tangent, band_usable, band_region = inputs
        usable_w = band_windows(band_usable)
        region_w = band_windows(band_region)

        def mapped(tokens):
            return block_tokens(tokens, usable_w, region_w, *matrices)
        result, result_tangent = jax.jvp(mapped, (band_windows(band_primal),), (band_windows(band_tangent),))
        return (band_grid(result), band_grid(result_tangent))
    outputs = lax.map(band_pass, (to_bands(primal), to_bands(tangent), to_bands(usable), to_bands(region)))
    return (from_bands(outputs[0]), from_bands(outputs[1]))

def rolled_by(array, direction):
    return jnp.roll(array, (direction * (WLAT // 2), direction * (WLON // 2)), axis=(1, 2))

def reference(fields, tangent_pick, key_mask, w_qkv, w_out, w_up, w_down):
    tangent = jax.nn.one_hot(tangent_pick, D, dtype=jnp.bfloat16)
    usable = key_mask.astype(jnp.bfloat16)
    flat_region = jnp.zeros((LEV, NLAT, NLON), jnp.int32)
    primal, tangent = apply_block(fields, tangent, usable, flat_region, (w_qkv[0], w_out[0], w_up[0], w_down[0]))
    lat_index = jnp.arange(NLAT, dtype=jnp.int32)
    edge = (lat_index >= NLAT - WLAT // 2).astype(jnp.int32)
    region = jnp.broadcast_to(edge[None, :, None], (LEV, NLAT, NLON))
    primal, tangent = apply_block(rolled_by(primal, -1), rolled_by(tangent, -1), rolled_by(usable, -1), region, (w_qkv[1], w_out[1], w_up[1], w_down[1]))
    return (rolled_by(primal, 1), rolled_by(tangent, 1))
```

```python
import functools

import jax
import jax.numpy as jnp
from jax import lax
from jax.experimental import pallas as pl
from jax.experimental.pallas import tpu as pltpu
from jax.sharding import PartitionSpec as P

HEADS = 8
WLAT = 6
WLON = 12
EPS = 1e-05
MASKED = -1000000000.0
ROOT_HALF = 0.7071067811865476
GAUSS = 0.3989422804014327


BF = jnp.bfloat16
F32 = jnp.float32


class Plan:
    def __init__(self, mesh, fields, w_qkv, w_down):
        self.nlat, self.nlon = mesh.shape["lat"], mesh.shape["lon"]
        self.lev, self.rows, self.cols, self.d = fields.shape
        assert self.cols == WLON and self.rows % WLAT == 0
        self.wins = self.rows // WLAT
        self.quarter = self.lev * (WLAT // 2) * (WLON // 2)
        self.half = 2 * self.quarter
        self.tok = 4 * self.quarter
        self.n = self.wins * self.tok
        self.kept = self.wins * self.half - self.quarter
        self.kept_pad = -(-(self.kept + self.wins) // 8) * 8
        self.top_pad = -(-(self.quarter + 1) // 8) * 8
        self.ff = w_down.shape[1] * self.nlon
        self.shard = w_qkv.shape[1]
        self.sub = w_down.shape[1] // self.shard
        self.split = self.nlat % 8 == 0 and self.shard % 64 == 0 and self.nlon > 1
        self.widths = {
            "qkv": w_qkv.shape[2],
            "out": self.d,
            "up": self.ff,
            "down": self.sub * self.d,
        }
        self.pairs = (self.nlon - 1) // 2
        self.middle = self.nlon % 2 == 0

    def full_shape(self, name):
        return {
            "qkv": (self.d, 3 * self.d),
            "out": (self.d, self.d),
            "up": (self.d, self.ff),
            "down": (self.ff, self.d),
        }[name]


def moved(x, plan, target):
    pairs = []
    for l in range(plan.nlat):
        for z in range(plan.nlon):
            tl, tz = target(l, z)
            pairs.append((l * plan.nlon + z, (tl % plan.nlat) * plan.nlon + tz % plan.nlon))
    return lax.ppermute(x, ("lat", "lon"), pairs)


def spread_columns(plan, shards):
    lat = lax.axis_index("lat")
    core, place = lat % 2, (lat // 2) % 4
    fourth = plan.shard // 4
    eighth = fourth // 2
    parts = []
    for name, shard in shards:
        if name == "down":
            for k in range(plan.sub):
                start = (place * plan.sub + k) * fourth
                parts.append(lax.dynamic_slice_in_dim(shard, start, fourth, axis=0))
        else:
            parts.append(lax.dynamic_slice_in_dim(shard, place * fourth, fourth, axis=0))
    whole = parts[0] if len(parts) == 1 else jnp.concatenate(parts, axis=1)
    got = []
    for p in range(1, plan.pairs + 1):
        got.append(
            moved(whole, plan, lambda l, z, p=p: (l, z + p) if l % 2 == 0 else (l, z - p))
        )
    if plan.middle:
        part = lax.dynamic_slice_in_dim(whole, core * eighth, eighth, axis=0)
        got.append(moved(part, plan, lambda l, z: (l, z + plan.nlon // 2)))
    return got[0] if len(got) == 1 else jnp.concatenate(got, axis=0)


def spread_plane(plan, mine):
    first = moved(mine, plan, lambda l, z: (l ^ 2, z) if l % 2 == 0 else (l ^ 4, z))
    second = moved(mine, plan, lambda l, z: (l ^ 4, z) if l % 2 == 0 else (l ^ 2, z))
    third = moved(first, plan, lambda l, z: (l ^ 4, z) if l % 2 == 0 else (l ^ 2, z))
    own = [mine, first, second, third]
    return own + [moved(x, plan, lambda l, z: (l ^ 1, z)) for x in own]


def start_weights(plan, block, names, shard_refs, piece_refs, dst_refs, sems):
    if not plan.split:
        for i, name in enumerate(names):
            pltpu.make_async_copy(piece_refs[i], dst_refs[i], sems.at[i]).start()
        return
    lat, lon = lax.axis_index("lat"), lax.axis_index("lon")
    n, fourth = plan.nlon, plan.shard // 4
    eighth = fourth // 2
    core, x, y = lat % 2, (lat // 2) % 2, (lat // 4) % 2
    for i, name in enumerate(names):
        rows = shard_refs[i].shape[1]
        at = pl.multiple_of(lon * rows, 16)
        pltpu.make_async_copy(
            shard_refs[i].at[block], dst_refs[i].at[pl.ds(at, rows)], sems.at[i]
        ).start()
    for half in (0, 1):
        c = core if half == 0 else 1 - core
        for j in range(4):
            ref = piece_refs[4 * half + j]
            flip_x = {0: 0, 3: 1}.get(j, (1 - c) if j == 1 else c)
            flip_y = {0: 0, 3: 1}.get(j, c if j == 1 else (1 - c))
            qx = x + flip_x - 2 * x * flip_x
            qy = y + flip_y - 2 * y * flip_y
            place = 2 * qy + qx
            groups = []
            for p in range(1, plan.pairs + 1):
                origin = lax.rem(lon + n - p + 2 * p * c, n)
                groups.append((fourth * (p - 1), fourth, origin, 0))
            if plan.middle:
                origin = lax.rem(lon + n // 2, n)
                groups.append((fourth * plan.pairs, eighth, origin, eighth * c))
            for src_row, count, origin, extra in groups:
                col = 0
                for i, name in enumerate(names):
                    if name == "down":
                        for k in range(plan.sub):
                            row = ((origin * 4 + place) * plan.sub + k) * fourth + extra
                            pltpu.make_async_copy(
                                ref.at[pl.ds(src_row, count), pl.ds(col, plan.d)],
                                dst_refs[i].at[pl.ds(pl.multiple_of(row, 8), count)],
                                sems.at[i],
                            ).start()
                            col += plan.d
                    else:
                        row = (origin * 4 + place) * fourth + extra
                        width = plan.widths[name]
                        pltpu.make_async_copy(
                            ref.at[pl.ds(src_row, count), pl.ds(col, width)],
                            dst_refs[i].at[pl.ds(pl.multiple_of(row, 8), count)],
                            sems.at[i],
                        ).start()
                        col += width


def wait_weights(dst_ref, sem):
    pltpu.make_async_copy(dst_ref, dst_ref, sem).wait()


def both_rows(ref, at, plan):
    return jnp.concatenate(
        [ref[pl.ds(at, plan.tok)], ref[pl.ds(pl.multiple_of(plan.n + at, 16), plan.tok)]], 0
    )


def project_qkv(plan, xd_ref, w_ref, packed_ref):
    for j in range(3):
        cols = pl.ds(j * plan.d, plan.d)

        @pl.loop(0, 2 * plan.wins)
        def _(w):
            rows = pl.ds(pl.multiple_of(w * plan.tok, 16), plan.tok)
            packed_ref[rows, cols] = jnp.dot(
                xd_ref[rows], w_ref[:, cols], preferred_element_type=F32
            ).astype(BF)


def attend(plan, w, packed_ref, keys, region_edge, att_ref):
    tok, d = plan.tok, plan.d
    size = d // HEADS
    wide = 2 * size
    at = pl.multiple_of(w * tok, 16)
    rows, drows = pl.ds(at, tok), pl.ds(pl.multiple_of(plan.n + at, 16), tok)
    qi = lax.broadcasted_iota(jnp.int32, (tok, tok), 0)
    ki = lax.broadcasted_iota(jnp.int32, (tok, tok), 1)
    allowed = jnp.broadcast_to(keys > 0.5, (tok, tok))
    if region_edge is not None:
        quarter, half = plan.quarter, plan.half

        def low(i):
            return ((i >= quarter) & (i < half)) | (i >= half + quarter)

        allowed = allowed & ((low(qi) == low(ki)) | jnp.logical_not(region_edge))
    allowed = allowed | (qi == ki)
    allowed = jnp.concatenate([allowed, allowed], 0)
    lane = lax.broadcasted_iota(jnp.int32, (1, wide), 1)
    pick_a = jnp.where(lane < size, size ** (-0.5), 0.0).astype(BF)
    pick_b = jnp.where(lane < size, 0.0, size ** (-0.5)).astype(BF)
    first = lax.broadcasted_iota(jnp.int32, (tok, wide), 1) < size
    zeros = jnp.zeros((tok, wide), BF)
    for p in range(HEADS // 2):
        def part(r, which):
            return packed_ref[r, pl.ds(which * d + p * wide, wide)]

        q, dq = part(rows, 0), part(drows, 0)
        k, dk = part(rows, 1), part(drows, 1)
        v, dv = part(rows, 2), part(drows, 2)
        qa, qb = q * pick_a, q * pick_b
        left = jnp.concatenate([qa, qb, dq * pick_a, dq * pick_b], 0)
        right = jnp.concatenate([zeros, zeros, qa, qb], 0)
        scores = lax.dot_general(
            jnp.concatenate([left, right], 1),
            jnp.concatenate([k, dk], 1),
            (((1,), (1,)), ((), ())),
            preferred_element_type=F32,
        )
        s, ds = scores[: 2 * tok], scores[2 * tok :]
        s = jnp.where(allowed, s, MASKED)
        e = jnp.exp(s - jnp.max(s, 1, keepdims=True))
        probs = e * (1.0 / jnp.sum(e, 1, keepdims=True))
        dprobs = probs * (ds - jnp.sum(probs * ds, 1, keepdims=True))
        mixed = jnp.dot(
            jnp.concatenate([probs, dprobs], 0).astype(BF),
            jnp.concatenate([v, dv], 1),
            preferred_element_type=F32,
        )
        pa, pb = mixed[:tok], mixed[tok : 2 * tok]
        da, db = mixed[2 * tok : 3 * tok], mixed[3 * tok :]
        cols = pl.ds(p * wide, wide)
        att_ref[rows, cols] = jnp.where(first, pa[:, :wide], pb[:, :wide]).astype(BF)
        att_ref[drows, cols] = jnp.where(
            first, da[:, :wide] + pa[:, wide:], db[:, :wide] + pb[:, wide:]
        ).astype(BF)


def norm_pair(v, dv):
    scale = 1.0 / v.shape[1]
    c = v - jnp.sum(v, 1, keepdims=True) * scale
    dc = dv - jnp.sum(dv, 1, keepdims=True) * scale
    r = lax.rsqrt(jnp.sum(c * c, 1, keepdims=True) * scale + EPS)
    cross = jnp.sum(c * dc, 1, keepdims=True) * scale
    y = c * r
    return y, (dc - y * (r * cross)) * r


def rest_of_block(plan, x, dx, att, w_out, w_up, w_down):
    tok, d = plan.tok, plan.d
    proj = jnp.dot(att, w_out[...], preferred_element_type=F32)
    y, dy = norm_pair(proj[:tok], proj[tok:])
    hidden, dhidden = x + y, dx + dy
    inner = jnp.concatenate([hidden, dhidden], 0).astype(BF)
    total = None
    for j in range(plan.ff // d):
        cols = pl.ds(j * d, d)
        up = jnp.dot(inner, w_up[:, cols], preferred_element_type=F32)
        u, du = up[:tok], up[tok:]
        cdf = 0.5 + 0.5 * lax.erf(u * ROOT_HALF)
        pdf = GAUSS * jnp.exp(-0.5 * (u * u))
        act = jnp.concatenate([u * cdf, du * (cdf + u * pdf)], 0).astype(BF)
        term = jnp.dot(act, w_down[cols], preferred_element_type=F32)
        total = term if total is None else total + term
    y, dy = norm_pair(total[:tok], total[tok:])
    return hidden + y, dhidden + dy


def seeds(plan, pick_ref, at):
    lane = lax.broadcasted_iota(jnp.int32, (plan.tok, plan.d), 1)
    return jnp.where(pick_ref[pl.ds(at, plan.tok)] == lane, 1.0, 0.0)


def first_attention(plan, n_pieces, *refs):
    fields, pick, masks, shard = refs[:4]
    pieces = refs[4 : 4 + n_pieces]
    x_out, att_out, xf, xd, packed, w_qkv, sems = refs[4 + n_pieces :]
    start_weights(plan, 0, ("qkv",), (shard,), pieces, (w_qkv,), sems)
    g = WLON // 2
    for w in range(plan.wins):
        for lev in range(plan.lev):
            for row in range(WLAT):
                line = fields[lev, w * WLAT + row].astype(F32)
                r, i = divmod(row, WLAT // 2)
                at = w * plan.tok + r * plan.quarter + (lev * (WLAT // 2) + i) * g
                xf[at : at + g] = line[:g]
                xf[at + plan.half : at + plan.half + g] = line[g:]
    for w in range(plan.wins):
        at = w * plan.tok
        x = xf[at : at + plan.tok].astype(BF)
        x_out[at : at + plan.tok] = x
        xd[at : at + plan.tok] = x
        xd[plan.n + at : plan.n + at + plan.tok] = seeds(plan, pick, at).astype(BF)
    wait_weights(w_qkv, sems.at[0])
    project_qkv(plan, xd, w_qkv, packed)

    @pl.loop(0, plan.wins)
    def _(w):
        keys = masks[w, :, : plan.tok]
        attend(plan, w, packed, keys, None, att_out)


def first_rest(plan, n_pieces, *refs):
    x_ref, att, pick, masks, s_out, s_up, s_down = refs[:7]
    pieces = refs[7 : 7 + n_pieces]
    kept_l, kept_r, top_l, top_r, flat, top, w_out, w_up, w_down, sems = refs[7 + n_pieces :]
    start_weights(
        plan, 0, ("out", "up", "down"), (s_out, s_up, s_down), pieces, (w_out, w_up, w_down), sems
    )
    wait_weights(w_out, sems.at[0])
    wait_weights(w_up, sems.at[1])
    wait_weights(w_down, sems.at[2])

    @pl.loop(0, plan.wins)
    def _(w):
        at = pl.multiple_of(w * plan.tok, 16)
        y = rest_of_block(
            plan,
            x_ref[pl.ds(at, plan.tok)].astype(F32),
            seeds(plan, pick, at),
            both_rows(att, at, plan),
            w_out,
            w_up,
            w_down,
        )
        to = pl.ds(pl.multiple_of(w * plan.half, 8), plan.half)
        for s in range(2):
            flat[s, 0, to] = y[s][: plan.half]
            flat[s, 1, to] = y[s][plan.half :]

    q, whole = plan.quarter, plan.wins * plan.half
    for c, (kept, tops) in enumerate(((kept_l, top_l), (kept_r, top_r))):
        for s in range(2):
            for i in range(plan.kept_pad - plan.kept):
                row = plan.wins + c * plan.wins + min(i, plan.wins - 1)
                flat[s, c, whole + i : whole + i + 1] = masks[row]
            kept[s] = flat[s, c, q : q + plan.kept_pad].astype(BF)
            top[0:q] = flat[s, c, 0:q]
            for i in range(plan.top_pad - q):
                top[q + i : q + i + 1] = masks[3 * plan.wins + c]
            tops[s] = top[...].astype(BF)


def second_block(plan, n_pieces, *refs):
    own, own_top, east, east_top, s_qkv, s_out, s_up, s_down = refs[:8]
    pieces = refs[8 : 8 + n_pieces]
    (keep_r, send_l, low_r, low_l, xd, packed, att, flat, seam,
     w_qkv, w_out, w_up, w_down, sems) = refs[8 + n_pieces :]
    start_weights(
        plan,
        1,
        ("qkv", "out", "up", "down"),
        (s_qkv, s_out, s_up, s_down),
        pieces,
        (w_qkv, w_out, w_up, w_down),
        sems,
    )
    q, half, tok = plan.quarter, plan.half, plan.tok
    for w in range(plan.wins):
        for s in range(2):
            for c, (kept, tops) in enumerate(((own, own_top), (east, east_top))):
                if w < plan.wins - 1:
                    seam[c * half : c * half + half] = kept[s, w * half : w * half + half].astype(F32)
                else:
                    last = kept[s, w * half : plan.kept_pad].astype(F32)
                    seam[c * half : c * half + q] = last[:q]
                    seam[c * half + q : c * half + half] = tops[s].astype(F32)[:q]
            at = s * plan.n + w * tok
            xd[at : at + tok] = seam[...].astype(BF)
    k = plan.kept
    base = (k // 8) * 8
    marks = own[0, base:].astype(F32) + east[0, base:].astype(F32)
    marks = marks[k - base : k - base + plan.wins]
    seam_t = (q // 8) * 8
    extra = own_top[0, seam_t:].astype(F32) + east_top[0, seam_t:].astype(F32)
    extra = extra[q - seam_t : q - seam_t + 1]
    wait_weights(w_qkv, sems.at[0])
    project_qkv(plan, xd, w_qkv, packed)
    edge = lax.axis_index("lat") == plan.nlat - 1
    for w in range(plan.wins):
        keys = marks[w : w + 1]
        if w == plan.wins - 1:
            keys = keys + extra
        attend(
            plan, w, packed, keys[:, :tok], edge if w == plan.wins - 1 else None, att
        )
    wait_weights(w_out, sems.at[1])
    wait_weights(w_up, sems.at[2])
    wait_weights(w_down, sems.at[3])

    @pl.loop(0, plan.wins)
    def _(w):
        at = pl.multiple_of(w * tok, 16)
        y = rest_of_block(
            plan,
            xd[pl.ds(at, tok)].astype(F32),
            xd[pl.ds(pl.multiple_of(plan.n + at, 16), tok)].astype(F32),
            both_rows(att, at, plan),
            w_out,
            w_up,
            w_down,
        )
        to = pl.ds(pl.multiple_of(w * half, 8), half)
        for s in range(2):
            flat[s, 0, to] = y[s][:half]
            flat[s, 1, to] = y[s][half:]

    for c, (kept, low) in enumerate(((keep_r, low_r), (send_l, low_l))):
        for s in range(2):
            kept[s] = flat[s, c, 0:k].astype(BF)
            low[s] = flat[s, c, k : k + q].astype(BF)


def join_halves(plan, left, left_top, right, right_top, primal, tangent, flat):
    q, g = plan.quarter, WLON // 2
    for s, out in enumerate((primal, tangent)):
        for c, (kept, top) in enumerate(((left, left_top), (right, right_top))):
            flat[c, 0:q] = top[s].astype(F32)
            flat[c, q : q + plan.kept] = kept[s].astype(F32)
        for lev in range(plan.lev):
            for row in range(plan.rows):
                w, r = divmod(row, WLAT)
                r, i = divmod(r, WLAT // 2)
                at = w * plan.half + r * q + (lev * (WLAT // 2) + i) * g
                out[lev, row] = jnp.concatenate(
                    [flat[0, at : at + g], flat[1, at : at + g]], 0
                ).astype(BF)


def call(body, plan, inputs, pieces, outs, scratch, flops, trans, name, any_inputs=0):
    vmem = pl.BlockSpec(memory_space=pltpu.VMEM)
    away = pl.BlockSpec(memory_space=pl.ANY)
    n_vmem = len(inputs) - any_inputs
    moved_bytes = sum(a.size * a.dtype.itemsize for a in (*inputs[:n_vmem], *pieces))
    moved_bytes += sum(a.size * a.dtype.itemsize for a in outs)
    return pl.pallas_call(
        body,
        out_shape=tuple(outs),
        in_specs=[vmem] * n_vmem + [away] * (any_inputs + len(pieces)),
        out_specs=tuple(vmem for _ in outs),
        scratch_shapes=scratch,
        compiler_params=pltpu.CompilerParams(vmem_limit_bytes=60 * 1024 * 1024),
        cost_estimate=pl.CostEstimate(
            flops=flops, bytes_accessed=moved_bytes, transcendentals=trans
        ),
        name=name,
    )(*inputs, *pieces)


def token_order(plan, a):
    s = a.reshape(plan.lev, plan.wins, 2, WLAT // 2, 2, WLON // 2)
    return s.transpose(1, 4, 2, 0, 3, 5).reshape(plan.wins, 2, 2, plan.quarter)


def mask_rows(plan, key_mask):
    m = token_order(plan, key_mask.astype(F32))
    rows = []

    def lanes(values, at):
        return jnp.pad(values, ((0, 0), (at, plan.d - at - values.shape[1])))

    rows.append(lanes(m.reshape(plan.wins, plan.tok), 0))
    for c in (0, 1):
        flat = m[:, c].reshape(plan.wins * plan.half)[plan.quarter :]
        flat = jnp.pad(flat, (0, plan.quarter)).reshape(plan.wins, plan.half)
        rows.append(lanes(flat, plan.half if c == 0 else 0))
    for c in (0, 1):
        at = (plan.half if c == 0 else 0) + plan.quarter
        rows.append(lanes(m[0:1, c, 0], at))
    return jnp.concatenate(rows, 0)[:, None, :]


def on_device(mesh, fields, tangent_pick, key_mask, w_qkv, w_out, w_up, w_down):
    plan = Plan(mesh, fields, w_qkv, w_down)
    d, n = plan.d, plan.n
    stacks = {"qkv": w_qkv, "out": w_out, "up": w_up, "down": w_down}
    phases = (
        (0, ("qkv",)),
        (0, ("out", "up", "down")),
        (1, ("qkv", "out", "up", "down")),
    )
    if plan.split:
        columns = [
            spread_columns(plan, [(name, stacks[name][b]) for name in names])
            for b, names in phases
        ]
        pieces = [spread_plane(plan, mine) for mine in columns]
    else:
        pieces = [
            [lax.all_gather(stacks[name][b], "lon", axis=0, tiled=True) for name in names]
            for b, names in phases
        ]
    pick = token_order(plan, tangent_pick).reshape(n, 1)
    masks = mask_rows(plan, key_mask)

    def shaped(shape, dtype=BF):
        return jax.ShapeDtypeStruct(shape, dtype)

    def weights(names):
        return [pltpu.VMEM(plan.full_shape(name), BF) for name in names]

    attn_flops = 2 * 2 * n * d * 3 * d + plan.wins * HEADS * 12 * plan.tok * plan.tok * 128
    rest_flops = 2 * 2 * n * (d * d + 2 * d * plan.ff)
    x, att = call(
        functools.partial(first_attention, plan, len(pieces[0])),
        plan,
        (fields, pick, masks, w_qkv),
        pieces[0],
        [shaped((n, d)), shaped((2 * n, d))],
        [
            pltpu.VMEM((n, d), F32),
            pltpu.VMEM((2 * n, d), BF),
            pltpu.VMEM((2 * n, 3 * d), BF),
            *weights(("qkv",)),
            pltpu.SemaphoreType.DMA((1,)),
        ],
        attn_flops,
        plan.wins * HEADS * plan.tok * plan.tok,
        "first_attention",
        any_inputs=1,
    )
    kept_l, kept_r, top_l, top_r = call(
        functools.partial(first_rest, plan, len(pieces[1])),
        plan,
        (x, att, pick, masks, w_out, w_up, w_down),
        pieces[1],
        [shaped((2, plan.kept_pad, d))] * 2 + [shaped((2, plan.top_pad, d))] * 2,
        [
            pltpu.VMEM((2, 2, plan.wins * plan.half + plan.kept_pad - plan.kept, d), F32),
            pltpu.VMEM((plan.top_pad, d), F32),
            *weights(("out", "up", "down")),
            pltpu.SemaphoreType.DMA((3,)),
        ],
        rest_flops,
        2 * n * plan.ff,
        "first_rest",
        any_inputs=3,
    )
    east = moved(kept_l, plan, lambda l, z: (l, z - 1))
    own_top = moved(top_r, plan, lambda l, z: (l - 1, z))
    east_top = moved(top_l, plan, lambda l, z: (l - 1, z - 1))
    keep_r, send_l, low_r, low_l = call(
        functools.partial(second_block, plan, len(pieces[2])),
        plan,
        (kept_r, own_top, east, east_top, w_qkv, w_out, w_up, w_down),
        pieces[2],
        [shaped((2, plan.kept, d))] * 2 + [shaped((2, plan.quarter, d))] * 2,
        [
            pltpu.VMEM((2 * n, d), BF),
            pltpu.VMEM((2 * n, 3 * d), BF),
            pltpu.VMEM((2 * n, d), BF),
            pltpu.VMEM((2, 2, plan.wins * plan.half, d), F32),
            pltpu.VMEM((plan.tok, d), F32),
            *weights(("qkv", "out", "up", "down")),
            pltpu.SemaphoreType.DMA((4,)),
        ],
        attn_flops + rest_flops,
        2 * n * plan.ff,
        "second_block",
        any_inputs=4,
    )
    left = moved(send_l, plan, lambda l, z: (l, z + 1))
    right_top = moved(low_r, plan, lambda l, z: (l + 1, z))
    left_top = moved(low_l, plan, lambda l, z: (l + 1, z + 1))
    return call(
        functools.partial(join_halves, plan),
        plan,
        (left, left_top, keep_r, right_top),
        [],
        [shaped(fields.shape)] * 2,
        [pltpu.VMEM((2, plan.wins * plan.half, d), F32)],
        0,
        0,
        "join_halves",
    )


def solution(mesh):
    rows = P(None, "lat", "lon", None)
    cells = P(None, "lat", "lon")
    held = P(None, "lon", None)
    return jax.shard_map(
        functools.partial(on_device, mesh),
        mesh=mesh,
        in_specs=(rows, cells, cells, held, held, held, held),
        out_specs=(rows, rows),
        check_vma=False,
    )
```
